32 devices in a mesh: rows: 4 (over y, core), chan: 8 (over z, x).
Axes of the slice: x: 2, y: 2, z: 4, core: 2. Of those that a mesh axis runs over, the one named last changes fastest.
Arguments:
- features: bfloat16 [1024, 16, 128], P('chan', 'rows'), may hold values from -6 to 6
- hidden: bfloat16 [1024, 16, 128], P('chan', 'rows'), may hold values from -1 to 1
- w_update: bfloat16 [3, 3, 1024, 2048], P(None, None, 'chan'), may hold values from -0.046875 to 0.046875
- w_reset: bfloat16 [3, 3, 1024, 2048], P(None, None, 'chan'), may hold values from -0.046875 to 0.046875
- w_cand: bfloat16 [3, 3, 1024, 2048], P(None, None, 'chan'), may hold values from -0.046875 to 0.046875
- b_update: float32 [1024], P('chan'), may hold values from -1 to 1
- b_reset: float32 [1024], P('chan'), may hold values from -1 to 1
- b_cand: float32 [1024], P('chan'), may hold values from -1 to 1
Outputs:
- new_hidden: bfloat16 [1024, 16, 128], P('chan', 'rows')
The draws below stay inside these ranges and needn't reach their ends.
All inputs are finite; a program needn't handle non-finite values.
Results may differ from the reference program's by a relative error of at most 0.0018.
Values may be sent and summed in bfloat16 or wider, within the bound.
A program may use at most 128 MiB of HBM per device.

```python
import jax
import jax.numpy as jnp
from jax import lax

C_IN = 1024
HID = 1024
COLS = 128
HEIGHT = 16


def level_of(own_key, extent, split, least, largest):
    factor_of, own = 1.0, jax.random.fold_in(own_key, 6)
    for position, parts in split:
        steps = jnp.exp(jax.random.uniform(jax.random.fold_in(own, position), (parts,), jnp.float32, least / len(split), largest / len(split)))
        factor_of = factor_of * jnp.repeat(steps, extent[position] // parts).reshape([-1 if axis == position else 1 for axis in range(len(extent))])
    return factor_of


def noise(key, shape, width, most, pieces=(), held_as=jnp.bfloat16):
    level = level_of(key, shape, pieces, -0.22, 0.18) if pieces else 1.0
    drawn = jax.random.normal(key, shape, jnp.float32) * width * level
    return jnp.minimum(jnp.maximum(drawn, -most), most).astype(held_as)


def setup_inputs(seed: int = 0) -> dict:
    arg_keys = jax.random.split(jax.random.key(seed), 9)
    features = noise(arg_keys[0], (C_IN, HEIGHT, COLS), 1.0, 6.0, ((0, 8), (1, 4)))
    hidden = jnp.clip(jax.random.uniform(arg_keys[1], (HID, HEIGHT, COLS), jnp.float32, -1.0, 1.0) * level_of(arg_keys[1], (HID, HEIGHT, COLS), ((0, 8), (1, 4)), -0.4, 0.0), -1.0, 1.0).astype(jnp.bfloat16)
    w_update = noise(arg_keys[2], (3, 3, HID, C_IN + HID), (9 * (C_IN + HID)) ** -0.5, 0.046875, ((2, 8),))
    w_reset = noise(arg_keys[3], (3, 3, HID, C_IN + HID), (9 * (C_IN + HID)) ** -0.5, 0.046875, ((2, 8),))
    w_cand = noise(arg_keys[4], (3, 3, HID, C_IN + HID), (9 * (C_IN + HID)) ** -0.5, 0.046875, ((2, 8),))
    b_update = jnp.clip(jax.random.uniform(arg_keys[5], (HID,), jnp.float32, -1.0, 1.0) * level_of(arg_keys[5], (HID,), ((0, 8),), -0.4, 0.0), -1.0, 1.0)
    b_reset = jnp.clip(jax.random.uniform(arg_keys[6], (HID,), jnp.float32, -1.0, 1.0) * level_of(arg_keys[6], (HID,), ((0, 8),), -0.4, 0.0), -1.0, 1.0)
    b_cand = jnp.clip(jax.random.uniform(arg_keys[7], (HID,), jnp.float32, -1.0, 1.0) * level_of(arg_keys[7], (HID,), ((0, 8),), -0.4, 0.0), -1.0, 1.0)
    return {"features": features, "hidden": hidden, "w_update": w_update, "w_reset": w_reset, "w_cand": w_cand, "b_update": b_update, "b_reset": b_reset, "b_cand": b_cand}


def conv_full(source, kernel):
    weights = jnp.transpose(kernel.astype(jnp.float32), (2, 3, 0, 1))
    result = lax.conv_general_dilated(source[None], weights, (1, 1), ((1, 1), (1, 1)), dimension_numbers=("NCHW", "OIHW", "NCHW"), precision=lax.Precision.HIGHEST)
    return result[0]


def reference(features, hidden, w_update, w_reset, w_cand, b_update, b_reset, b_cand):
    joined = jnp.concatenate([features, hidden], 0).astype(jnp.float32)
    update = jax.nn.sigmoid(conv_full(joined, w_update) + b_update[:, None, None])
    reset = jax.nn.sigmoid(conv_full(joined, w_reset) + b_reset[:, None, None])
    hidden_f = hidden.astype(jnp.float32)
    reset_hidden = (reset * hidden_f).astype(jnp.bfloat16)
    second = jnp.concatenate([features.astype(jnp.float32), reset_hidden.astype(jnp.float32)], 0)
    candidate = jnp.tanh(conv_full(second, w_cand) + b_cand[:, None, None])
    return ((1.0 - update) * hidden_f + update * candidate).astype(jnp.bfloat16)
```

```python
import functools

import jax
import jax.numpy as jnp
from jax import lax
from jax.experimental import pallas as pl
from jax.experimental.pallas import tpu as pltpu
from jax.sharding import PartitionSpec as P

MESH = pl.DeviceIdType.MESH
PAIR = 2


def kernel(
    n_chan, n_rows, cols,
    loc, bias, w_update, w_reset, w_cand,
    out,
    joined, rh, rh_loc, weights, acc, acc_cand, gate,
    w_sem, own_sem, send1, band1, rim1, send2, band2, rim2,
):
    n = loc.shape[1]
    band = loc.shape[2]
    channels = joined.shape[1]
    lines = n_chan // PAIR
    me = lax.axis_index("chan")
    row = lax.axis_index("rows")
    line, pair = me // PAIR, me % PAIR
    has_up, has_down = line < lines - 1, line > 0
    has_above, has_below = row > 0, row < n_rows - 1

    w_copies = [
        pltpu.make_async_copy(src, weights.at[i], w_sem.at[i])
        for i, src in enumerate((w_reset, w_update, w_cand))
    ]
    for copy in w_copies:
        copy.start()

    def ident(l, p):
        return l * PAIR + p

    up, down, partner = ident(line + 1, pair), ident(line - 1, pair), ident(line, 1 - pair)
    barrier = pltpu.get_barrier_semaphore()

    def greet(there, target):
        @pl.when(there)
        def _():
            pl.semaphore_signal(barrier, inc=1, device_id=target, device_id_type=MESH)

    pl.semaphore_signal(barrier, inc=1, device_id={"chan": partner}, device_id_type=MESH)
    greet(has_up, {"chan": up})
    greet(has_down, {"chan": down})
    greet(has_above, {"rows": row - 1})
    greet(has_below, {"rows": row + 1})
    pl.semaphore_wait(
        barrier,
        1
        + has_up.astype(jnp.int32)
        + has_down.astype(jnp.int32)
        + has_above.astype(jnp.int32)
        + has_below.astype(jnp.int32),
    )

    def mover(own, buf, send, band_sem, rim_sem):
        def place(c):
            return pl.ds(pl.multiple_of(c * n, n), n)

        def band_copy(kind, c, mine, target):
            dst = buf.at[:, place(c), pl.ds(cols, band)]
            return pltpu.make_async_remote_copy(
                src_ref=own if mine else dst,
                dst_ref=dst,
                send_sem=send.at[kind, c],
                recv_sem=band_sem.at[c],
                device_id={"chan": target},
                device_id_type=MESH,
            )

        def rim_copy(side, c, mine):
            start = 0 if side == 0 else band - cols
            src = (
                own.at[:, :, pl.ds(start, cols)]
                if mine
                else buf.at[:, place(c), pl.ds(cols + start, cols)]
            )
            dst_col = cols + band if side == 0 else 0
            return pltpu.make_async_remote_copy(
                src_ref=src,
                dst_ref=buf.at[:, place(c), pl.ds(dst_col, cols)],
                send_sem=send.at[3 + side, c],
                recv_sem=rim_sem.at[side, c],
                device_id={"rows": row - 1 if side == 0 else row + 1},
                device_id_type=MESH,
            )

        def rims(c, mine, act):
            @pl.when(has_above)
            def _():
                act(rim_copy(0, c, mine))

            @pl.when(has_below)
            def _():
                act(rim_copy(1, c, mine))

        def start(copy):
            copy.start()

        def done(copy):
            copy.wait_send()

        def send_up(c, mine, act):
            @pl.when(has_up)
            def _():
                act(band_copy(0, c, mine, up))

        def send_down(c, mine, act):
            @pl.when(has_down)
            def _():
                act(band_copy(1, c, mine, down))

        def local():
            return pltpu.make_async_copy(
                own, buf.at[:, place(me), pl.ds(cols, band)], own_sem
            )

        def begin(act):
            band_copy(2, me, True, partner).start() if act is start else band_copy(
                2, me, True, partner
            ).wait_send()
            send_up(me, True, act)
            send_down(me, True, act)
            rims(me, True, act)

        def from_below(s, act, first):
            c = ident(line - s, pair)

            @pl.when(line >= s)
            def _():
                if first:
                    band_copy(0, c, False, partner).wait_recv()
                act(band_copy(2, c, False, partner))
                send_up(c, False, act)
                rims(c, False, act)

        def from_above(s, act, first):
            c = ident(line + s, pair)

            @pl.when(line + s < lines)
            def _():
                if first:
                    band_copy(0, c, False, partner).wait_recv()
                act(band_copy(2, c, False, partner))
                send_down(c, False, act)
                rims(c, False, act)

        def from_pair(l, ok, act, first):
            c = ident(l, 1 - pair)

            @pl.when(ok)
            def _():
                if first:
                    band_copy(2, c, False, partner).wait_recv()
                rims(c, False, act)

        def ready(c):
            @pl.when(has_below)
            def _():
                rim_copy(0, c, False).wait_recv()

            @pl.when(has_above)
            def _():
                rim_copy(1, c, False).wait_recv()

        def across(s, act, first):
            from_pair(line - s, line >= s, act, first)
            if s > 0:
                from_pair(line + s, line + s < lines, act, first)

        def run(compute):
            eager = n % 128 == 0

            def use(s, p):
                if not eager:
                    return
                for l, ok in (
                    (line - s, line >= s),
                    (line + s, line + s < lines),
                )[: 1 if s == 0 else 2]:
                    @pl.when(ok)
                    def _():
                        c = ident(l, p)
                        ready(c)
                        compute(c)

            local().wait()
            for s in range(1, lines):
                from_below(s, start, True)
                from_above(s, start, True)
                across(s - 1, start, True)
                use(s - 1, pair)
                if s >= 2:
                    use(s - 2, 1 - pair)
            across(lines - 1, start, True)
            if lines >= 2:
                use(lines - 2, 1 - pair)
            use(lines - 1, pair)
            use(lines - 1, 1 - pair)
            if not eager:
                for c in range(n_chan):
                    ready(c)
                for g in range(channels // 128):
                    compute(g)

        def finish():
            begin(done)
            for s in range(1, lines):
                from_below(s, done, False)
                from_above(s, done, False)
            for s in range(lines):
                across(s, done, False)

        def launch():
            begin(start)
            local().start()

        return launch, run, finish

    launch1, run1, finish1 = mover(loc, joined, send1, band1, rim1)
    launch2, run2, finish2 = mover(rh_loc, rh, send2, band2, rim2)
    launch1()

    @pl.when(jnp.logical_not(has_above))
    def _():
        for buf in (joined, rh):
            buf[:, :, pl.ds(0, cols)] = jnp.zeros((buf.shape[0], channels, cols), buf.dtype)

    @pl.when(jnp.logical_not(has_below))
    def _():
        for buf in (joined, rh):
            buf[:, :, pl.ds(cols + band, cols)] = jnp.zeros(
                (buf.shape[0], channels, cols), buf.dtype
            )

    def part(gates, parts, ks_list, buf, bufs, g):
        ks = pl.ds(pl.multiple_of(g * 128, 128), 128)
        left, right = [], []
        for a in range(3):
            for offset, b in zip(ks_list, bufs):
                kw = pl.ds(pl.multiple_of(offset + g * 128, 128), 128)
                w = weights[pl.ds(gates, parts), a, :, :, kw]
                left.append(w.reshape(parts * 3 * n, 128))
                right.append(buf[b, ks, pl.ds(a * cols, band)])
        return jnp.dot(
            jnp.concatenate(left, 1),
            jnp.concatenate(right, 0),
            preferred_element_type=jnp.float32,
        )

    acc[...] = jnp.zeros_like(acc)
    for copy in w_copies:
        copy.wait()

    def gates_on(g):
        for i in range(2):
            acc[i] += part(i, 1, (0, channels), joined, (0, 1), g)

    run1(gates_on)

    lane = lax.broadcasted_iota(jnp.int32, (n, cols), 1)

    def folded(ref, i, r):
        cells = pl.ds(r * cols, cols)
        low = pltpu.roll(ref[i, pl.ds(0, n), cells], 1, 1)
        mid = ref[i, pl.ds(n, n), cells]
        high = pltpu.roll(ref[i, pl.ds(2 * n, n), cells], cols - 1, 1)
        return jnp.where(lane == 0, 0.0, low) + mid + jnp.where(lane == cols - 1, 0.0, high)

    for r in range(band // cols):
        cells = pl.ds(r * cols, cols)
        reset = jax.nn.sigmoid(folded(acc, 0, r) + bias[1])
        rh_loc[0, :, cells] = (reset * loc[1, :, cells].astype(jnp.float32)).astype(rh_loc.dtype)
    launch2()

    for r in range(band // cols):
        gate[:, pl.ds(r * cols, cols)] = jax.nn.sigmoid(folded(acc, 1, r) + bias[0])
    acc_cand[0] = part(2, 1, (0,), joined, (0,), 0)

    @pl.loop(1, channels // 128)
    def _(g):
        acc_cand[0] += part(2, 1, (0,), joined, (0,), g)

    def cand_on(g):
        acc_cand[0] += part(2, 1, (channels,), rh, (0,), g)

    run2(cand_on)

    for r in range(band // cols):
        cells = pl.ds(r * cols, cols)
        candidate = jnp.tanh(folded(acc_cand, 0, r) + bias[2])
        update = gate[:, cells]
        out[:, cells] = (
            (1.0 - update) * loc[1, :, cells].astype(jnp.float32) + update * candidate
        ).astype(out.dtype)
    finish1()
    finish2()


def per_device(n_chan, n_rows, features, hidden, w_update, w_reset, w_cand, b_update, b_reset, b_cand):
    n, rows, cols = features.shape
    band = rows * cols
    channels = n * n_chan
    wide = band + 2 * cols
    loc = jnp.stack([features.reshape(n, band), hidden.reshape(n, band)])
    bias = jnp.stack([b_update, b_reset, b_cand])[:, :, None]
    bf16, f32 = jnp.bfloat16, jnp.float32
    vmem = pl.BlockSpec(memory_space=pltpu.VMEM)
    hbm = pl.BlockSpec(memory_space=pl.ANY)
    dma = pltpu.SemaphoreType.DMA
    result = pl.pallas_call(
        functools.partial(kernel, n_chan, n_rows, cols),
        out_shape=jax.ShapeDtypeStruct((n, band), bf16),
        in_specs=[vmem, vmem, hbm, hbm, hbm],
        out_specs=vmem,
        scratch_shapes=[
            pltpu.VMEM((2, channels, wide), bf16),
            pltpu.VMEM((1, channels, wide), bf16),
            pltpu.VMEM((1, n, band), bf16),
            pltpu.VMEM((3,) + w_update.shape, bf16),
            pltpu.VMEM((2, 3 * n, band), f32),
            pltpu.VMEM((1, 3 * n, band), f32),
            pltpu.VMEM((n, band), f32),
            dma((3,)),
            dma,
            dma((5, n_chan)),
            dma((n_chan,)),
            dma((2, n_chan)),
            dma((5, n_chan)),
            dma((n_chan,)),
            dma((2, n_chan)),
        ],
        compiler_params=pltpu.CompilerParams(
            collective_id=0, has_side_effects=True, vmem_limit_bytes=60 * 1024 * 1024
        ),
    )(loc, bias, w_update, w_reset, w_cand)
    return result.reshape(n, rows, cols)


def solution(mesh):
    in_specs = (
        P("chan", "rows", None),
        P("chan", "rows", None),
        P(None, None, "chan", None),
        P(None, None, "chan", None),
        P(None, None, "chan", None),
        P("chan"),
        P("chan"),
        P("chan"),
    )
    return jax.shard_map(
        functools.partial(per_device, mesh.shape["chan"], mesh.shape["rows"]),
        mesh=mesh,
        in_specs=in_specs,
        out_specs=P("chan", "rows", None),
        check_vma=False,
    )
```

```python
import functools

import jax
import jax.numpy as jnp
from jax import lax
from jax.experimental import pallas as pl
from jax.experimental.pallas import tpu as pltpu
from jax.sharding import PartitionSpec as P

MESH = pl.DeviceIdType.MESH
PAIR = 2


def kernel(
    n_chan, n_rows, cols,
    features, hidden, b_update, b_reset, b_cand, w_update, w_reset, w_cand,
    out,
    joined, rh, rh_loc, weights, acc, acc_cand, gate,
    w_sem, own_sem, send1, band1, rim1, send2, band2, rim2,
):
    n = features.shape[0]
    band = features.shape[1]
    channels = joined.shape[1]
    lines = n_chan // PAIR
    me = lax.axis_index("chan")
    row = lax.axis_index("rows")
    line, pair = me // PAIR, me % PAIR
    has_up, has_down = line < lines - 1, line > 0
    has_above, has_below = row > 0, row < n_rows - 1

    w_copies = [
        pltpu.make_async_copy(src, weights.at[i], w_sem.at[i])
        for i, src in enumerate((w_reset, w_update, w_cand))
    ]
    for copy in w_copies:
        copy.start()

    def ident(l, p):
        return l * PAIR + p

    up, down, partner = ident(line + 1, pair), ident(line - 1, pair), ident(line, 1 - pair)
    barrier = pltpu.get_barrier_semaphore()

    def greet(there, target):
        @pl.when(there)
        def _():
            pl.semaphore_signal(barrier, inc=1, device_id=target, device_id_type=MESH)

    pl.semaphore_signal(barrier, inc=1, device_id={"chan": partner}, device_id_type=MESH)
    greet(has_up, {"chan": up})
    greet(has_down, {"chan": down})
    greet(has_above, {"rows": row - 1})
    greet(has_below, {"rows": row + 1})
    pl.semaphore_wait(
        barrier,
        1
        + has_up.astype(jnp.int32)
        + has_down.astype(jnp.int32)
        + has_above.astype(jnp.int32)
        + has_below.astype(jnp.int32),
    )

    def mover(own, dest, own_sem, send, band_sem, rim_sem):
        def band_copy(kind, c, h, mine, target):
            dst = dest(c, h, cols, band)
            return pltpu.make_async_remote_copy(
                src_ref=own(h, 0, band) if mine else dst,
                dst_ref=dst,
                send_sem=send.at[kind, c, h],
                recv_sem=band_sem.at[c, h],
                device_id={"chan": target},
                device_id_type=MESH,
            )

        def rim_copy(side, c, h, mine):
            first = 0 if side == 0 else band - cols
            return pltpu.make_async_remote_copy(
                src_ref=own(h, first, cols) if mine else dest(c, h, cols + first, cols),
                dst_ref=dest(c, h, cols + band if side == 0 else 0, cols),
                send_sem=send.at[3 + side, c, h],
                recv_sem=rim_sem.at[side, c, h],
                device_id={"rows": row - 1 if side == 0 else row + 1},
                device_id_type=MESH,
            )

        def start(copy):
            copy.start()

        def done(copy):
            copy.wait_send()

        def rims(c, h, mine, act):
            @pl.when(has_above)
            def _():
                act(rim_copy(0, c, h, mine))

            @pl.when(has_below)
            def _():
                act(rim_copy(1, c, h, mine))

        def send_line(kind, ok, c, h, mine, act):
            @pl.when(ok)
            def _():
                act(band_copy(kind, c, h, mine, up if kind == 0 else down))

        def local(h):
            return pltpu.make_async_copy(own(h, 0, band), dest(me, h, cols, band), own_sem.at[h])

        def begin(act):
            for h in range(2):
                send_line(0, has_up, me, h, True, act)
                send_line(1, has_down, me, h, True, act)
                act(band_copy(2, me, h, True, partner))
            for h in range(2):
                rims(me, h, True, act)

        def from_below(s, h, act, first):
            c = ident(line - s, pair)

            @pl.when(line >= s)
            def _():
                if first:
                    band_copy(0, c, h, False, partner).wait_recv()
                send_line(0, has_up, c, h, False, act)
                act(band_copy(2, c, h, False, partner))
                rims(c, h, False, act)

        def from_above(s, h, act, first):
            c = ident(line + s, pair)

            @pl.when(line + s < lines)
            def _():
                if first:
                    band_copy(0, c, h, False, partner).wait_recv()
                send_line(1, has_down, c, h, False, act)
                act(band_copy(2, c, h, False, partner))
                rims(c, h, False, act)

        def from_pair(l, ok, act, first):
            c = ident(l, 1 - pair)

            @pl.when(ok)
            def _():
                for h in range(2):
                    if first:
                        band_copy(2, c, h, False, partner).wait_recv()
                    rims(c, h, False, act)

        def ready(c):
            for h in range(2):
                @pl.when(has_below)
                def _():
                    rim_copy(0, c, h, False).wait_recv()

                @pl.when(has_above)
                def _():
                    rim_copy(1, c, h, False).wait_recv()

        def across(s, act, first):
            from_pair(line - s, line >= s, act, first)
            if s > 0:
                from_pair(line + s, line + s < lines, act, first)

        def run(compute):
            eager = n % 128 == 0

            def use(s, p):
                if not eager:
                    return
                for l, ok in (
                    (line - s, line >= s),
                    (line + s, line + s < lines),
                )[: 1 if s == 0 else 2]:
                    @pl.when(ok)
                    def _():
                        c = ident(l, p)
                        ready(c)
                        compute(c)

            for h in range(2):
                local(h).wait()
            for s in range(1, lines):
                for h in range(2):
                    from_below(s, h, start, True)
                    from_above(s, h, start, True)
                across(s - 1, start, True)
                use(s - 1, pair)
                if s >= 2:
                    use(s - 2, 1 - pair)
            if lines >= 2:
                use(lines - 2, 1 - pair)
            use(lines - 1, pair)
            across(lines - 1, start, True)
            use(lines - 1, 1 - pair)
            if not eager:
                for c in range(n_chan):
                    ready(c)
                for g in range(channels // 128):
                    compute(g)

        def finish():
            begin(done)
            for s in range(1, lines):
                for h in range(2):
                    from_below(s, h, done, False)
                    from_above(s, h, done, False)
            for s in range(lines):
                across(s, done, False)

        def launch():
            begin(start)
            for h in range(2):
                local(h).start()

        return launch, run, finish

    def own1(h, start, size):
        return (features, hidden)[h].at[:, pl.ds(start, size)]

    def dest1(c, h, start, size):
        return joined.at[h, pl.ds(pl.multiple_of(c * n, n), n), pl.ds(start, size)]

    half = n // 2

    def own2(h, start, size):
        return rh_loc.at[pl.ds(h * half, half), pl.ds(start, size)]

    def dest2(c, h, start, size):
        return rh.at[
            0, pl.ds(pl.multiple_of(c * n + h * half, half), half), pl.ds(start, size)
        ]

    launch1, run1, finish1 = mover(own1, dest1, own_sem.at[0], send1, band1, rim1)
    launch2, run2, finish2 = mover(own2, dest2, own_sem.at[1], send2, band2, rim2)
    launch1()

    @pl.when(jnp.logical_not(has_above))
    def _():
        for buf in (joined, rh):
            buf[:, :, pl.ds(0, cols)] = jnp.zeros((buf.shape[0], channels, cols), buf.dtype)

    @pl.when(jnp.logical_not(has_below))
    def _():
        for buf in (joined, rh):
            buf[:, :, pl.ds(cols + band, cols)] = jnp.zeros(
                (buf.shape[0], channels, cols), buf.dtype
            )

    def part(gates, parts, ks_list, buf, bufs, g):
        ks = pl.ds(pl.multiple_of(g * 128, 128), 128)
        left, right = [], []
        for a in range(3):
            for offset, b in zip(ks_list, bufs):
                kw = pl.ds(pl.multiple_of(offset + g * 128, 128), 128)
                w = weights[pl.ds(gates, parts), a, :, :, kw]
                left.append(w.reshape(parts * 3 * n, 128))
                right.append(buf[b, ks, pl.ds(a * cols, band)])
        return jnp.dot(
            jnp.concatenate(left, 1),
            jnp.concatenate(right, 0),
            preferred_element_type=jnp.float32,
        )

    acc[...] = jnp.zeros_like(acc)
    for copy in w_copies:
        copy.wait()

    def gates_on(g):
        for i in range(2):
            acc[i] += part(i, 1, (0, channels), joined, (0, 1), g)

    run1(gates_on)

    lane = lax.broadcasted_iota(jnp.int32, (n, cols), 1)

    diagonal = lax.broadcasted_iota(jnp.int32, (n, n), 0) == lax.broadcasted_iota(
        jnp.int32, (n, n), 1
    )

    def column(ref):
        return jnp.sum(jnp.where(diagonal, ref[...], 0.0), axis=1, keepdims=True)

    def folded(ref, i, r):
        cells = pl.ds(r * cols, cols)
        low = pltpu.roll(ref[i, pl.ds(0, n), cells], 1, 1)
        mid = ref[i, pl.ds(n, n), cells]
        high = pltpu.roll(ref[i, pl.ds(2 * n, n), cells], cols - 1, 1)
        return jnp.where(lane == 0, 0.0, low) + mid + jnp.where(lane == cols - 1, 0.0, high)

    for r in range(band // cols):
        cells = pl.ds(r * cols, cols)
        reset = jax.nn.sigmoid(folded(acc, 0, r) + column(b_reset))
        rh_loc[:, cells] = (reset * hidden[:, cells].astype(jnp.float32)).astype(rh_loc.dtype)
    launch2()

    for r in range(band // cols):
        gate[:, pl.ds(r * cols, cols)] = jax.nn.sigmoid(folded(acc, 1, r) + column(b_update))
    acc_cand[0] = part(2, 1, (0,), joined, (0,), 0)

    @pl.loop(1, channels // 128)
    def _(g):
        acc_cand[0] += part(2, 1, (0,), joined, (0,), g)

    def cand_on(g):
        acc_cand[0] += part(2, 1, (channels,), rh, (0,), g)

    run2(cand_on)

    for r in range(band // cols):
        cells = pl.ds(r * cols, cols)
        candidate = jnp.tanh(folded(acc_cand, 0, r) + column(b_cand))
        update = gate[:, cells]
        out[:, cells] = (
            (1.0 - update) * hidden[:, cells].astype(jnp.float32) + update * candidate
        ).astype(out.dtype)
    finish1()
    finish2()


def per_device(n_chan, n_rows, features, hidden, w_update, w_reset, w_cand, b_update, b_reset, b_cand):
    n, rows, cols = features.shape
    band = rows * cols
    channels = n * n_chan
    wide = band + 2 * cols
    bf16, f32 = jnp.bfloat16, jnp.float32
    vmem = pl.BlockSpec(memory_space=pltpu.VMEM)
    hbm = pl.BlockSpec(memory_space=pl.ANY)
    dma = pltpu.SemaphoreType.DMA
    result = pl.pallas_call(
        functools.partial(kernel, n_chan, n_rows, cols),
        out_shape=jax.ShapeDtypeStruct((n, band), bf16),
        in_specs=[vmem] * 5 + [hbm] * 3,
        out_specs=vmem,
        scratch_shapes=[
            pltpu.VMEM((2, channels, wide), bf16),
            pltpu.VMEM((1, channels, wide), bf16),
            pltpu.VMEM((n, band), bf16),
            pltpu.VMEM((3,) + w_update.shape, bf16),
            pltpu.VMEM((2, 3 * n, band), f32),
            pltpu.VMEM((1, 3 * n, band), f32),
            pltpu.VMEM((n, band), f32),
            dma((3,)),
            dma((2, 2)),
            dma((5, n_chan, 2)),
            dma((n_chan, 2)),
            dma((2, n_chan, 2)),
            dma((5, n_chan, 2)),
            dma((n_chan, 2)),
            dma((2, n_chan, 2)),
        ],
        compiler_params=pltpu.CompilerParams(
            collective_id=0, has_side_effects=True, vmem_limit_bytes=60 * 1024 * 1024
        ),
    )(
        features.reshape(n, band),
        hidden.reshape(n, band),
        b_update.reshape(1, n),
        b_reset.reshape(1, n),
        b_cand.reshape(1, n),
        w_update,
        w_reset,
        w_cand,
    )
    return result.reshape(n, rows, cols)


def solution(mesh):
    in_specs = (
        P("chan", "rows", None),
        P("chan", "rows", None),
        P(None, None, "chan", None),
        P(None, None, "chan", None),
        P(None, None, "chan", None),
        P("chan"),
        P("chan"),
        P("chan"),
    )
    return jax.shard_map(
        functools.partial(per_device, mesh.shape["chan"], mesh.shape["rows"]),
        mesh=mesh,
        in_specs=in_specs,
        out_specs=P("chan", "rows", None),
        check_vma=False,
    )
```

```python
import functools

import jax
import jax.numpy as jnp
from jax import lax
from jax.experimental import pallas as pl
from jax.experimental.pallas import tpu as pltpu
from jax.sharding import PartitionSpec as P

MESH = pl.DeviceIdType.MESH
PAIR = 2


def kernel(
    n_chan, n_rows, cols,
    features, hidden, b_update, b_reset, b_cand, w_update, w_reset, w_cand,
    out,
    joined, rh, rh_loc, weights, acc, acc_cand, gate,
    w_sem, own_sem, send1, band1, rim1, send2, band2, rim2,
):
    n = features.shape[0]
    band = features.shape[1]
    channels = joined.shape[1]
    lines = n_chan // PAIR
    me = lax.axis_index("chan")
    row = lax.axis_index("rows")
    line, pair = me // PAIR, me % PAIR
    has_up, has_down = line < lines - 1, line > 0
    has_above, has_below = row > 0, row < n_rows - 1

    w_copies = [
        pltpu.make_async_copy(src, weights.at[i], w_sem.at[i])
        for i, src in enumerate((w_reset, w_update, w_cand))
    ]
    for copy in w_copies:
        copy.start()

    def ident(l, p):
        return l * PAIR + p

    up, down, partner = ident(line + 1, pair), ident(line - 1, pair), ident(line, 1 - pair)
    barrier = pltpu.get_barrier_semaphore()

    def greet(there, target):
        @pl.when(there)
        def _():
            pl.semaphore_signal(barrier, inc=1, device_id=target, device_id_type=MESH)

    pl.semaphore_signal(barrier, inc=1, device_id={"chan": partner}, device_id_type=MESH)
    greet(has_up, {"chan": up})
    greet(has_down, {"chan": down})
    greet(has_above, {"rows": row - 1})
    greet(has_below, {"rows": row + 1})
    pl.semaphore_wait(
        barrier,
        1
        + has_up.astype(jnp.int32)
        + has_down.astype(jnp.int32)
        + has_above.astype(jnp.int32)
        + has_below.astype(jnp.int32),
    )

    def mover(own, dest, own_sem, send, band_sem, rim_sem):
        def band_copy(kind, c, h, mine, target):
            dst = dest(c, h, cols, band)
            return pltpu.make_async_remote_copy(
                src_ref=own(h, 0, band) if mine else dst,
                dst_ref=dst,
                send_sem=send.at[kind, c, h],
                recv_sem=band_sem.at[c, h],
                device_id={"chan": target},
                device_id_type=MESH,
            )

        def rim_copy(side, c, h, mine):
            first = 0 if side == 0 else band - cols
            return pltpu.make_async_remote_copy(
                src_ref=own(h, first, cols) if mine else dest(c, h, cols + first, cols),
                dst_ref=dest(c, h, cols + band if side == 0 else 0, cols),
                send_sem=send.at[3 + side, c, h],
                recv_sem=rim_sem.at[side, c, h],
                device_id={"rows": row - 1 if side == 0 else row + 1},
                device_id_type=MESH,
            )

        def start(copy):
            copy.start()

        def done(copy):
            copy.wait_send()

        def rims(c, h, mine, act):
            @pl.when(has_above)
            def _():
                act(rim_copy(0, c, h, mine))

            @pl.when(has_below)
            def _():
                act(rim_copy(1, c, h, mine))

        def send_line(kind, ok, c, h, mine, act):
            @pl.when(ok)
            def _():
                act(band_copy(kind, c, h, mine, up if kind == 0 else down))

        def local(h):
            return pltpu.make_async_copy(own(h, 0, band), dest(me, h, cols, band), own_sem.at[h])

        def begin(act):
            for h in range(2):
                send_line(0, has_up, me, h, True, act)
                send_line(1, has_down, me, h, True, act)
                act(band_copy(2, me, h, True, partner))
            for h in range(2):
                rims(me, h, True, act)

        def from_below(s, h, act, first):
            c = ident(line - s, pair)

            @pl.when(line >= s)
            def _():
                if first:
                    band_copy(0, c, h, False, partner).wait_recv()
                send_line(0, has_up, c, h, False, act)
                act(band_copy(2, c, h, False, partner))
                rims(c, h, False, act)

        def from_above(s, h, act, first):
            c = ident(line + s, pair)

            @pl.when(line + s < lines)
            def _():
                if first:
                    band_copy(0, c, h, False, partner).wait_recv()
                send_line(1, has_down, c, h, False, act)
                act(band_copy(2, c, h, False, partner))
                rims(c, h, False, act)

        def from_pair(l, ok, act, first):
            c = ident(l, 1 - pair)

            @pl.when(ok)
            def _():
                for h in range(2):
                    if first:
                        band_copy(2, c, h, False, partner).wait_recv()
                    rims(c, h, False, act)

        def ready(c):
            for h in range(2):
                @pl.when(has_below)
                def _():
                    rim_copy(0, c, h, False).wait_recv()

                @pl.when(has_above)
                def _():
                    rim_copy(1, c, h, False).wait_recv()

        def across(s, act, first):
            from_pair(line - s, line >= s, act, first)
            if s > 0:
                from_pair(line + s, line + s < lines, act, first)

        def run(compute):
            eager = n % 128 == 0

            def use(s, p):
                if not eager:
                    return
                for l, ok in (
                    (line - s, line >= s),
                    (line + s, line + s < lines),
                )[: 1 if s == 0 else 2]:
                    @pl.when(ok)
                    def _():
                        c = ident(l, p)
                        ready(c)
                        compute(c)

            for h in range(2):
                local(h).wait()
            for s in range(1, lines):
                from_below(s, 0, start, True)
                from_above(s, 0, start, True)
                across(s - 1, start, True)
                from_below(s, 1, start, True)
                from_above(s, 1, start, True)
                use(s - 1, pair)
                if s >= 2:
                    use(s - 2, 1 - pair)
            if lines >= 2:
                use(lines - 2, 1 - pair)
            use(lines - 1, pair)
            across(lines - 1, start, True)
            use(lines - 1, 1 - pair)
            if not eager:
                for c in range(n_chan):
                    ready(c)
                for g in range(channels // 128):
                    compute(g)

        def finish():
            begin(done)
            for s in range(1, lines):
                for h in range(2):
                    from_below(s, h, done, False)
                    from_above(s, h, done, False)
            for s in range(lines):
                across(s, done, False)

        def launch():
            begin(start)
            for h in range(2):
                local(h).start()

        return launch, run, finish

    def own1(h, start, size):
        return (features, hidden)[h].at[:, pl.ds(start, size)]

    def dest1(c, h, start, size):
        return joined.at[h, pl.ds(pl.multiple_of(c * n, n), n), pl.ds(start, size)]

    half = n // 2

    def own2(h, start, size):
        return rh_loc.at[pl.ds(h * half, half), pl.ds(start, size)]

    def dest2(c, h, start, size):
        return rh.at[
            0, pl.ds(pl.multiple_of(c * n + h * half, half), half), pl.ds(start, size)
        ]

    launch1, run1, finish1 = mover(own1, dest1, own_sem.at[0], send1, band1, rim1)
    launch2, run2, finish2 = mover(own2, dest2, own_sem.at[1], send2, band2, rim2)
    launch1()

    @pl.when(jnp.logical_not(has_above))
    def _():
        for buf in (joined, rh):
            buf[:, :, pl.ds(0, cols)] = jnp.zeros((buf.shape[0], channels, cols), buf.dtype)

    @pl.when(jnp.logical_not(has_below))
    def _():
        for buf in (joined, rh):
            buf[:, :, pl.ds(cols + band, cols)] = jnp.zeros(
                (buf.shape[0], channels, cols), buf.dtype
            )

    def part(gates, parts, ks_list, buf, bufs, g):
        ks = pl.ds(pl.multiple_of(g * 128, 128), 128)
        left, right = [], []
        for a in range(3):
            for offset, b in zip(ks_list, bufs):
                kw = pl.ds(pl.multiple_of(offset + g * 128, 128), 128)
                w = weights[pl.ds(gates, parts), a, :, :, kw]
                left.append(w.reshape(parts * 3 * n, 128))
                right.append(buf[b, ks, pl.ds(a * cols, band)])
        return jnp.dot(
            jnp.concatenate(left, 1),
            jnp.concatenate(right, 0),
            preferred_element_type=jnp.float32,
        )

    acc[...] = jnp.zeros_like(acc)
    for copy in w_copies:
        copy.wait()

    def gates_on(g):
        for i in range(2):
            acc[i] += part(i, 1, (0, channels), joined, (0, 1), g)

    run1(gates_on)

    lane = lax.broadcasted_iota(jnp.int32, (n, cols), 1)

    diagonal = lax.broadcasted_iota(jnp.int32, (n, n), 0) == lax.broadcasted_iota(
        jnp.int32, (n, n), 1
    )

    def column(ref):
        return jnp.sum(jnp.where(diagonal, ref[...], 0.0), axis=1, keepdims=True)

    def folded(ref, i, r):
        cells = pl.ds(r * cols, cols)
        low = pltpu.roll(ref[i, pl.ds(0, n), cells], 1, 1)
        mid = ref[i, pl.ds(n, n), cells]
        high = pltpu.roll(ref[i, pl.ds(2 * n, n), cells], cols - 1, 1)
        return jnp.where(lane == 0, 0.0, low) + mid + jnp.where(lane == cols - 1, 0.0, high)

    for r in range(band // cols):
        cells = pl.ds(r * cols, cols)
        reset = jax.nn.sigmoid(folded(acc, 0, r) + column(b_reset))
        rh_loc[:, cells] = (reset * hidden[:, cells].astype(jnp.float32)).astype(rh_loc.dtype)
    launch2()

    for r in range(band // cols):
        gate[:, pl.ds(r * cols, cols)] = jax.nn.sigmoid(folded(acc, 1, r) + column(b_update))
    acc_cand[0] = part(2, 1, (0,), joined, (0,), 0)

    @pl.loop(1, channels // 128)
    def _(g):
        acc_cand[0] += part(2, 1, (0,), joined, (0,), g)

    def cand_on(g):
        acc_cand[0] += part(2, 1, (channels,), rh, (0,), g)

    run2(cand_on)

    for r in range(band // cols):
        cells = pl.ds(r * cols, cols)
        candidate = jnp.tanh(folded(acc_cand, 0, r) + column(b_cand))
        update = gate[:, cells]
        out[:, cells] = (
            (1.0 - update) * hidden[:, cells].astype(jnp.float32) + update * candidate
        ).astype(out.dtype)
    finish1()
    finish2()


def per_device(n_chan, n_rows, features, hidden, w_update, w_reset, w_cand, b_update, b_reset, b_cand):
    n, rows, cols = features.shape
    band = rows * cols
    channels = n * n_chan
    wide = band + 2 * cols
    bf16, f32 = jnp.bfloat16, jnp.float32
    vmem = pl.BlockSpec(memory_space=pltpu.VMEM)
    hbm = pl.BlockSpec(memory_space=pl.ANY)
    dma = pltpu.SemaphoreType.DMA
    result = pl.pallas_call(
        functools.partial(kernel, n_chan, n_rows, cols),
        out_shape=jax.ShapeDtypeStruct((n, band), bf16),
        in_specs=[vmem] * 5 + [hbm] * 3,
        out_specs=vmem,
        scratch_shapes=[
            pltpu.VMEM((2, channels, wide), bf16),
            pltpu.VMEM((1, channels, wide), bf16),
            pltpu.VMEM((n, band), bf16),
            pltpu.VMEM((3,) + w_update.shape, bf16),
            pltpu.VMEM((2, 3 * n, band), f32),
            pltpu.VMEM((1, 3 * n, band), f32),
            pltpu.VMEM((n, band), f32),
            dma((3,)),
            dma((2, 2)),
            dma((5, n_chan, 2)),
            dma((n_chan, 2)),
            dma((2, n_chan, 2)),
            dma((5, n_chan, 2)),
            dma((n_chan, 2)),
            dma((2, n_chan, 2)),
        ],
        compiler_params=pltpu.CompilerParams(
            collective_id=0, has_side_effects=True, vmem_limit_bytes=60 * 1024 * 1024
        ),
    )(
        features.reshape(n, band),
        hidden.reshape(n, band),
        b_update.reshape(1, n),
        b_reset.reshape(1, n),
        b_cand.reshape(1, n),
        w_update,
        w_reset,
        w_cand,
    )
    return result.reshape(n, rows, cols)


def solution(mesh):
    in_specs = (
        P("chan", "rows", None),
        P("chan", "rows", None),
        P(None, None, "chan", None),
        P(None, None, "chan", None),
        P(None, None, "chan", None),
        P("chan"),
        P("chan"),
        P("chan"),
    )
    return jax.shard_map(
        functools.partial(per_device, mesh.shape["chan"], mesh.shape["rows"]),
        mesh=mesh,
        in_specs=in_specs,
        out_specs=P("chan", "rows", None),
        check_vma=False,
    )
```
